32 devices in a mesh: dp: 16 (over z, x, core), mp: 2 (over y).
Axes of the slice: x: 2, y: 2, z: 4, core: 2. Of those that a mesh axis runs over, the one named last changes fastest.
Arguments:
- images: bfloat16 [64, 196, 512], P('dp'), may hold values from -6 to 6
- cotangent: bfloat16 [64, 196, 512], P('dp'), may hold values from -6 to 6
- w_query: bfloat16 [512, 512], P('dp', 'mp'), may hold values from -0.25 to 0.25
- w_key: bfloat16 [512, 512], P('dp', 'mp'), may hold values from -0.25 to 0.25
- w_value: bfloat16 [512, 512], P('dp', 'mp'), may hold values from -0.25 to 0.25
- w_proj: bfloat16 [512, 512], P('mp', 'dp'), may hold values from -1 to 1
- w_up: bfloat16 [512, 2048], P('dp', 'mp'), may hold values from -0.25 to 0.25
- w_down: bfloat16 [2048, 512], P('mp', 'dp'), may hold values from -0.125 to 0.125
- gains: bfloat16 [2, 512], P(None, 'dp'), may hold values from 0.25 to 1.75
- shifts: bfloat16 [4, 512], P(None, 'dp'), may hold values from -3 to 3
- qv_bias: bfloat16 [2, 512], P(None, 'mp'), may hold values from -3 to 3
- up_bias: bfloat16 [2048], P('mp'), may hold values from -3 to 3
- table: bfloat16 [16, 169], P('mp'), may hold values from -5 to 5
- regions: int32 [4, 49], replicated, may hold values from 0 to 3
- rel_index: int32 [49, 49], replicated, may hold values from 0 to 168
Outputs:
- output: bfloat16 [64, 196, 512], P('dp')
- d_images: bfloat16 [64, 196, 512], P('dp')
- g_query: float32 [512, 512], P('dp', 'mp')
- g_key: float32 [512, 512], P('dp', 'mp')
- g_value: float32 [512, 512], P('dp', 'mp')
- g_proj: float32 [512, 512], P('mp', 'dp')
- g_up: float32 [512, 2048], P('dp', 'mp')
- g_down: float32 [2048, 512], P('mp', 'dp')
- g_gains: float32 [2, 512], P(None, 'dp')
- g_shifts: float32 [4, 512], P(None, 'dp')
- g_qv_bias: float32 [2, 512], P(None, 'mp')
- g_up_bias: float32 [2048], P('mp')
- g_table: float32 [16, 169], P('mp')
The draws below stay inside these ranges and needn't reach their ends.
Inputs may be any that keep to these rules, and one draw needn't show every extreme that they name: `regions`: a position's scores to positions of another region of its window get -100.
All inputs are finite; a program needn't handle non-finite values.
Results may differ from the reference program's by a relative error of at most 0.017.
Values may be sent and summed in bfloat16 or wider, within the bound.
No kernel may reach another device: no remote copies, remote signals or barrier semaphores. Data moves between devices by JAX's collectives and lax.ppermute only.
A program may use at most 128 MiB of HBM per device.

```python
import jax
import jax.numpy as jnp
from jax import lax

D = 512
HEADS = 16
HEAD_DIM = 32
FF = 2048
SIDE = 14
WIN = 7
SHIFT = 3
IMG_TOK = 196
WIN_TOK = 49
WINDOWS = 4
TABLE = 169
IMAGES = 64
N_DP = 16


def place_ends(array, key, least, top_value):
    place = [jax.random.randint(jax.random.fold_in(key, axis), (), 0, length) for axis, length in enumerate(array.shape)]
    longest = array.shape.index(max(array.shape))
    next_to = place[:longest] + [(place[longest] + 1) % array.shape[longest]] + place[longest + 1:]
    return array.at[tuple(place)].set(least).at[tuple(next_to)].set(top_value)


def with_spikes(entries, stream_key, source, target, parts, factor):
    owner, partner = [(jnp.arange(entries.shape[axis_at]) // (entries.shape[axis_at] // parts)).reshape([-1 if axis == axis_at else 1 for axis in range(entries.ndim)]) for axis_at in (source, target)]
    chosen = jax.random.permutation(stream_key, parts)[partner]
    strong = (owner == chosen) | (owner == (partner + parts // 2) % parts)
    return jnp.where(strong, factor * entries, entries)


def levels(stream_key, extent, split, least, top_value):
    def one(dim, blocks):
        heights = jax.random.uniform(jax.random.fold_in(jax.random.fold_in(stream_key, 6), dim), (blocks,), jnp.float32, least / len(split), top_value / len(split))
        return jnp.repeat(jnp.exp(heights), extent[dim] // blocks).reshape((-1,) + (1,) * (len(extent) - dim - 1))

    gain = one(*split[0])
    for cut in split[1:]:
        gain = gain * one(*cut)
    return gain


def normal_values(rng, extent, deviation, most, shards=(), kind=jnp.bfloat16):
    factor_of = levels(rng, extent, shards, -0.22, 0.18) if shards else 1.0
    array = jax.random.normal(rng, extent, jnp.float32) * deviation * factor_of
    return jnp.minimum(jnp.maximum(array, -most), most).astype(kind)


def heavy_noise(key, extent, deviation, limit, split, heavy, held_as=jnp.bfloat16):
    array = deviation * jax.random.normal(key, extent, jnp.float32)
    if split:
        array = array * levels(key, extent, split, -0.22, 0.18)
    return jnp.clip(with_spikes(array, jax.random.fold_in(key, 3), *heavy), -limit, limit).astype(held_as)


def setup_inputs(seed: int = 0) -> dict:
    splits = jax.random.split(jax.random.key(seed), 16)
    return {
        "images": heavy_noise(splits[0], (IMAGES, IMG_TOK, D), 1.0, 6.0, ((0, 16),), (0, 2, 16, 2.0)),
        "cotangent": heavy_noise(splits[1], (IMAGES, IMG_TOK, D), 1.0, 6.0, ((0, 16),), (0, 2, 16, 2.0)),
        "w_query": normal_values(splits[2], (D, D), D ** -0.5, 0.25, ((0, 16), (1, 2))),
        "w_key": normal_values(splits[3], (D, D), D ** -0.5, 0.25, ((0, 16), (1, 2))),
        "w_value": normal_values(splits[4], (D, D), D ** -0.5, 0.25, ((0, 16), (1, 2))),
        "w_proj": normal_values(splits[5], (D, D), (D // 16) ** -0.5, 1.0, ((0, 2), (1, 16))),
        "w_up": normal_values(splits[6], (D, FF), D ** -0.5, 0.25, ((0, 16), (1, 2))),
        "w_down": normal_values(splits[7], (FF, D), FF ** -0.5, 0.125, ((0, 2), (1, 16))),
        "gains": jnp.clip(1.0 + 0.15 * jax.random.normal(splits[8], (2, D), jnp.float32), 0.25, 1.75).astype(jnp.bfloat16),
        "shifts": normal_values(splits[9], (4, D), 0.5, 3.0, ((1, 16),)),
        "qv_bias": normal_values(splits[10], (2, D), 0.5, 3.0, ((1, 2),)),
        "up_bias": normal_values(splits[11], (FF,), 0.5, 3.0, ((0, 2),)),
        "table": normal_values(splits[12], (HEADS, TABLE), 1.0, 5.0, ((0, 2),)),
        "regions": place_ends(jax.random.randint(splits[13], (WINDOWS, WIN_TOK), 0, 4), jax.random.fold_in(splits[13], 1), 0, 3).astype(jnp.int32),
        "rel_index": place_ends(jax.random.randint(splits[14], (WIN_TOK, WIN_TOK), 0, TABLE), jax.random.fold_in(splits[14], 1), 0, TABLE - 1).astype(jnp.int32),
    }


@jax.custom_vjp
def low(v):
    return lax.optimization_barrier(v.astype(jnp.bfloat16)).astype(jnp.float32)

@jax.custom_vjp
def low_back(v):
    return v

def low_keep(v):
    return (low(v), None)

def low_pass(kept, grad):
    return (grad,)

def back_keep(v):
    return (v, None)

def back_low(kept, grad):
    return (low(grad),)
low.defvjp(low_keep, low_pass)
low_back.defvjp(back_keep, back_low)

def to_windows(source):
    image_count = source.shape[0]
    channels = source.shape[2]
    grid = source.reshape(image_count, SIDE, SIDE, channels)
    grid = jnp.roll(grid, (-SHIFT, -SHIFT), (1, 2))
    grid = grid.reshape(image_count, SIDE // WIN, WIN, SIDE // WIN, WIN, channels)
    return grid.transpose(0, 1, 3, 2, 4, 5).reshape(image_count * WINDOWS, WIN * WIN, channels)

def from_windows(source, image_count):
    channels = source.shape[2]
    grid = source.reshape(image_count, SIDE // WIN, SIDE // WIN, WIN, WIN, channels)
    grid = grid.transpose(0, 1, 3, 2, 4, 5).reshape(image_count, SIDE, SIDE, channels)
    grid = jnp.roll(grid, (SHIFT, SHIFT), (1, 2))
    return grid.reshape(image_count, SIDE * SIDE, channels)

def layer_norm(source, gain_row, shift_row):
    centred = source - lax.optimization_barrier(jnp.mean(source, axis=-1, keepdims=True))
    spread = lax.optimization_barrier(jnp.mean(centred * centred, axis=-1, keepdims=True))
    return centred * lax.rsqrt(spread + 1e-05) * gain_row + shift_row

def attend_core(queries, key_rows, values, rel_bias, region_mask):
    window_tokens = WIN * WIN
    query_heads = queries.reshape(-1, window_tokens, HEADS, HEAD_DIM)
    key_heads = key_rows.reshape(-1, window_tokens, HEADS, HEAD_DIM)
    value_heads = values.reshape(-1, window_tokens, HEADS, HEAD_DIM)
    scores = low_back(jnp.einsum('wihd,wjhd->whij', query_heads, key_heads, precision=lax.Precision.HIGHEST) * HEAD_DIM ** (-0.5))
    logits = scores.reshape(-1, WINDOWS, HEADS, window_tokens, window_tokens) + region_mask[None, :, None] + rel_bias[None, None]
    soft = jax.nn.softmax(logits, axis=-1)
    soft_low = low(soft).reshape(-1, HEADS, window_tokens, window_tokens)
    mixed = jnp.einsum('whij,wjhd->wihd', soft_low, value_heads, precision=lax.Precision.HIGHEST)
    return mixed.reshape(-1, HEADS * HEAD_DIM)

def forward(source, w_query, w_key, w_value, w_proj, w_up, w_down, gains, shifts, qv_bias, up_bias, table, onehot, region_mask):
    image_count = source.shape[0]
    row_count = image_count * SIDE * SIDE
    normed = low(layer_norm(source, gains[0], shifts[0]))
    window_rows = to_windows(normed).reshape(row_count, D)
    queries = low(low_back(jnp.dot(window_rows, w_query, precision=lax.Precision.HIGHEST) + qv_bias[0]))
    key_rows = low(low_back(jnp.dot(window_rows, w_key, precision=lax.Precision.HIGHEST)))
    values = low(low_back(jnp.dot(window_rows, w_value, precision=lax.Precision.HIGHEST) + qv_bias[1]))
    rel_bias = jnp.dot(table, onehot, precision=lax.Precision.HIGHEST).reshape(HEADS, WIN * WIN, WIN * WIN)
    mixed_out = low(low_back(jax.checkpoint(attend_core)(queries, key_rows, values, rel_bias, region_mask)))
    token_mixed = from_windows(mixed_out.reshape(image_count * WINDOWS, WIN * WIN, D), image_count).reshape(row_count, D)
    branch = low_back(jnp.dot(token_mixed, w_proj, precision=lax.Precision.HIGHEST)) + shifts[2]
    middle = source + branch.reshape(source.shape)
    normed_two = low(layer_norm(middle, gains[1], shifts[1])).reshape(row_count, D)
    hidden = low_back(jnp.dot(normed_two, w_up, precision=lax.Precision.HIGHEST) + up_bias)
    active = low(jax.nn.gelu(hidden, approximate=False))
    outward = low_back(jnp.dot(active, w_down, precision=lax.Precision.HIGHEST)) + shifts[3]
    return middle + outward.reshape(source.shape)

def reference(images, cotangent, w_query, w_key, w_value, w_proj, w_up, w_down, gains, shifts, qv_bias, up_bias, table, regions, rel_index):
    table_codes = jnp.arange(TABLE, dtype=jnp.int32)
    onehot = (rel_index.reshape(1, -1).astype(jnp.int32) == table_codes[:, None]).astype(jnp.float32)
    region_mask = jnp.where(regions[:, :, None] == regions[:, None, :], 0.0, -100.0).astype(jnp.float32)
    params = jax.tree.map(lambda weight_arr: weight_arr.astype(jnp.float32), (w_query, w_key, w_value, w_proj, w_up, w_down, gains, shifts, qv_bias, up_bias, table))
    group_in = images.astype(jnp.float32).reshape(N_DP, -1, SIDE * SIDE, D)
    group_grad = cotangent.astype(jnp.float32).reshape(N_DP, -1, SIDE * SIDE, D)

    def wrapped(source_arg, *weight_args):
        return forward(source_arg, *weight_args, onehot, region_mask)

    def one_group(totals, group_pair):
        source, cot_group = group_pair
        result, pull_back = jax.vjp(wrapped, source, *params)
        grads_all = pull_back(cot_group)
        totals = jax.tree.map(lambda left_val, right_val: left_val + right_val, totals, tuple(grads_all[1:]))
        return (totals, (result.astype(jnp.bfloat16), grads_all[0].astype(jnp.bfloat16)))
    starts = jax.tree.map(jnp.zeros_like, params)
    totals, (results, input_grads) = lax.scan(one_group, starts, (group_in, group_grad))
    return (results.reshape(IMAGES, SIDE * SIDE, D), input_grads.reshape(IMAGES, SIDE * SIDE, D), totals[0], totals[1], totals[2], totals[3], totals[4], totals[5], totals[6], totals[7], totals[8], totals[9], totals[10])
```

```python
import math

import jax
import jax.numpy as jnp
from jax import lax
from jax.experimental import pallas as pl
from jax.experimental.pallas import tpu as pltpu
from jax.sharding import PartitionSpec as P

HEAD_DIM = 32
SIDE = 14
WIN = 7
SHIFT = 3
WINDOWS = 4
TOKENS = WIN * WIN
PAD = 64
TILE = 128
HPT = TILE // HEAD_DIM
F32 = jnp.float32
BF16 = jnp.bfloat16
AXES = ("dp", "mp")


def nn(a, b):
    return lax.dot_general(a, b, (((1,), (0,)), ((), ())), preferred_element_type=F32)


def nt(a, b):
    return lax.dot_general(a, b, (((1,), (1,)), ((), ())), preferred_element_type=F32)


def tn(a, b):
    return lax.dot_general(a, b, (((0,), (0,)), ((), ())), preferred_element_type=F32)


def unit_of(v):
    centred = v - jnp.mean(v, axis=-1, keepdims=True)
    inverse = lax.rsqrt(jnp.mean(centred * centred, axis=-1, keepdims=True) + 1e-05)
    return centred * inverse, inverse


def norm_back(grad_in, unit_rows, inverse, gain_row):
    scaled = grad_in * gain_row
    return inverse * (
        scaled
        - jnp.mean(scaled, axis=-1, keepdims=True)
        - unit_rows * jnp.mean(scaled * unit_rows, axis=-1, keepdims=True)
    )


class Links:
    def __init__(self, ndp, nmp):
        self.ndp, self.nmp = ndp, nmp
        dp_bits = [1 << b for b in range(ndp.bit_length() - 1)]
        mp_bits = [1 << b for b in range(nmp.bit_length() - 1)]
        stages = []
        high = dp_bits[2:]
        while high:
            stages.append(self.combos([(b, 0) for b in high[-2:]]))
            high = high[:-2]
        if len(dp_bits) > 1:
            stages.append([(dp_bits[1], 0)])
        left = list(mp_bits)
        while left:
            stages.append(self.combos([(0, b) for b in left[:2]]))
            left = left[2:]
        if dp_bits:
            stages.append([(dp_bits[0], 0)])
        self.stages = stages
        deltas = [(0, 0)]
        for group in stages:
            deltas = deltas + [(a ^ o[0], b ^ o[1]) for o in group for a, b in deltas]
        self.deltas = deltas

    @staticmethod
    def combos(gens):
        out = [(0, 0)]
        for g in gens:
            out = out + [(a ^ g[0], b ^ g[1]) for a, b in out]
        return out[1:]

    def swap(self, x, offset):
        pairs = []
        for d in range(self.ndp):
            for m in range(self.nmp):
                pairs.append(
                    (d * self.nmp + m, (d ^ offset[0]) * self.nmp + (m ^ offset[1]))
                )
        return lax.ppermute(x, AXES, pairs)

    def gather(self, block):
        buf = block[None]
        for group in self.stages[:-1]:
            buf = jnp.concatenate([buf] + [self.swap(buf, o) for o in group], axis=0)
        return [buf] + [self.swap(buf, o) for o in self.stages[-1]]

    def scatter(self, parts):
        for at in range(len(self.stages) - 1, -1, -1):
            group = self.stages[at]
            got = [self.swap(p, o) for p, o in zip(parts[1:], group)]
            if at == 0:
                total = parts[0].astype(F32)
                for g in got:
                    total = total + g.astype(F32)
                return total[0]
            n = parts[0].shape[0] // (len(self.stages[at - 1]) + 1)
            fresh = []
            for b in range(len(self.stages[at - 1]) + 1):
                piece = parts[0][b * n : (b + 1) * n].astype(F32)
                for g in got:
                    piece = piece + g[b * n : (b + 1) * n].astype(F32)
                fresh.append(piece.astype(BF16))
            parts = fresh

    def total(self, x):
        for group in reversed(self.stages):
            got = [self.swap(x, o) for o in group]
            for g in got:
                x = x + g
        return x

    def over_mp(self, x):
        buf = x[None]
        bit = 1
        while bit < self.nmp:
            buf = jnp.concatenate([buf, self.swap(buf, (0, bit))], axis=0)
            bit *= 2
        return buf


def load_slots(ids, deltas, pieces, dst, sems, rows):
    per = len(deltas) // len(pieces)
    copies = []
    for j, (dd, dm) in enumerate(deltas):
        d = lax.bitwise_xor(ids[0], dd)
        m = lax.bitwise_xor(ids[1], dm)
        copies.append(
            pltpu.make_async_copy(
                pieces[j // per].at[j % per],
                dst.at[m, pl.ds(pl.multiple_of(d * rows, rows), rows), :],
                sems.at[j],
            )
        )
    for c in copies:
        c.start()
    return copies


def store_slots(ids, deltas, src, pieces, sems, rows):
    per = len(deltas) // len(pieces)
    copies = []
    for j, (dd, dm) in enumerate(deltas):
        d = lax.bitwise_xor(ids[0], dd)
        m = lax.bitwise_xor(ids[1], dm)
        copies.append(
            pltpu.make_async_copy(
                src.at[m, pl.ds(pl.multiple_of(d * rows, rows), rows), :],
                pieces[j // per].at[j % per],
                sems.at[j],
            )
        )
    for c in copies:
        c.start()
    return copies


def finish(copies):
    for c in copies:
        c.wait()


def head_mask():
    row = lax.broadcasted_iota(jnp.int32, (HPT * PAD, TILE), 0) // PAD
    lane = lax.broadcasted_iota(jnp.int32, (HPT * PAD, TILE), 1) // HEAD_DIM
    return row == lane


def spread(x, mask):
    stacked = jnp.concatenate([x] * HPT, axis=0)
    return jnp.where(mask, stacked, jnp.zeros_like(stacked))


def fold(x, mask):
    x = jnp.where(mask, x, 0.0)
    out = x[:PAD]
    for h in range(1, HPT):
        out = out + x[h * PAD : (h + 1) * PAD]
    return out


def attention_forward(deltas, nmp, lw, rows, windows, tiles):
    scale = HEAD_DIM**-0.5

    def kernel(ids, x_img, perm, qk_lo, qk_hi, vp_lo, vp_hi, qvb, bias, rmask,
               xw_o, q_o, k_o, v_o, p_o, mixed_o, middle_o, gs_o, wqk, wvp, sems):
        a = load_slots(ids, deltas, (qk_lo, qk_hi), wqk, sems.at[0], rows)
        b = load_slots(ids, deltas, (vp_lo, vp_hi), wvp, sems.at[1], rows)
        xw = nn(perm[...], x_img[...])
        xw_o[...] = xw.astype(BF16)
        unit, _ = unit_of(xw)
        finish(a)
        finish(b)
        gs = wqk[0, :, 2 * lw : 2 * lw + 128].astype(F32).T
        gs_o[...] = gs[:8]
        xn = (unit * gs[0:1] + gs[2:3]).astype(BF16)
        for m in range(nmp):
            cols = slice(m * lw, (m + 1) * lw)
            q_o[:, cols] = (nn(xn, wqk[m, :, 0:lw]) + qvb[0:1, cols]).astype(BF16)
            k_o[:, cols] = nn(xn, wqk[m, :, lw : 2 * lw]).astype(BF16)
            v_o[:, cols] = (nn(xn, wvp[m, :, 0:lw]) + qvb[1:2, cols]).astype(BF16)
        mask = head_mask()

        def one(w, carry):
            at = pl.ds(pl.multiple_of(w * PAD, PAD), PAD)
            area = jnp.concatenate([rmask[w]] * HPT, axis=0)
            for t in range(tiles):
                cols = slice(t * TILE, (t + 1) * TILE)
                raw = nt(spread(q_o[at, cols], mask), k_o[at, cols])
                logits = raw * scale + bias[t * HPT * PAD : (t + 1) * HPT * PAD, :] + area
                top = jnp.max(logits, axis=-1, keepdims=True)
                e = jnp.exp(logits - top)
                probs = e / jnp.sum(e, axis=-1, keepdims=True)
                p_o[w * tiles + t] = probs
                got = nn(probs.astype(BF16), v_o[at, cols])
                mixed_o[at, cols] = fold(got, mask).astype(BF16)
            return carry

        lax.fori_loop(0, windows, one, 0)
        total = xw + gs[4:5]
        for m in range(nmp):
            total = total + nt(mixed_o[:, m * lw : (m + 1) * lw], wvp[m, :, lw : 2 * lw])
        middle_o[...] = total

    return kernel


def feed_forward(deltas, nmp, fw, rows, chunk):
    root = 1.0 / math.sqrt(2.0)
    root_pi = 1.0 / math.sqrt(2.0 * math.pi)

    def kernel(ids, cot_img, perm, middle, gs, up_lo, up_hi, dn_lo, dn_hi, upb,
               out_o, gm_o, small_o, gup_lo, gup_hi, gdn_lo, gdn_hi,
               wup, wdn, gup, gdn, sems):
        a = load_slots(ids, deltas, (up_lo, up_hi), wup, sems.at[0], rows)
        b = load_slots(ids, deltas, (dn_lo, dn_hi), wdn, sems.at[1], rows)
        cot = nn(perm[...], cot_img[...])
        cot_low = cot.astype(BF16)
        mid = middle[...]
        unit, inverse = unit_of(mid)
        normed = (unit * gs[1:2] + gs[3:4]).astype(BF16)
        finish(a)
        finish(b)
        out = mid + gs[5:6]
        lifted = jnp.zeros_like(mid)
        small_o[...] = jnp.zeros(small_o.shape, F32)
        for m in range(nmp):
            for c in range(0, fw, chunk):
                cols = slice(c, c + chunk)
                first = m * fw + c
                hidden = nn(normed, wup[m, :, cols]) + upb[0:1, first : first + chunk]
                cdf = 0.5 * (1.0 + lax.erf(hidden * root))
                active = (hidden * cdf).astype(BF16)
                slope = cdf + hidden * (jnp.exp(-0.5 * hidden * hidden) * root_pi)
                out = out + nt(active, wdn[m, :, cols])
                gh32 = nn(cot_low, wdn[m, :, cols]) * slope
                gh = gh32.astype(BF16)
                lifted = lifted + nt(gh, wup[m, :, cols])
                gup[m, :, cols] = tn(normed, gh).astype(BF16)
                gdn[m, :, cols] = tn(cot_low, active).astype(BF16)
                small_o[4 + first // 512 : 5 + first // 512, first % 512 : first % 512 + chunk] = (
                    jnp.sum(gh.astype(F32), axis=0, keepdims=True)
                )
        a = store_slots(ids, deltas, gup, (gup_lo, gup_hi), sems.at[0], rows)
        b = store_slots(ids, deltas, gdn, (gdn_lo, gdn_hi), sems.at[1], rows)
        out_o[...] = tn(perm[...], out.astype(BF16)).astype(BF16)
        gm = cot + norm_back(lifted, unit, inverse, gs[1:2])
        gm_o[...] = gm
        small_o[0:1] = jnp.sum(lifted * unit, axis=0, keepdims=True)
        small_o[1:2] = jnp.sum(lifted, axis=0, keepdims=True)
        small_o[2:3] = jnp.sum(gm, axis=0, keepdims=True)
        small_o[3:4] = jnp.sum(cot, axis=0, keepdims=True)
        finish(a)
        finish(b)

    return kernel


def attention_backward(deltas, nmp, lw, rows, windows, tiles):
    scale = HEAD_DIM**-0.5

    def kernel(ids, xw, perm, wqk, wvp, q, k, v, probs, mixed, gm, gs,
               dimg_o, small_o, ds_o, gqk_lo, gqk_hi, gvp_lo, gvp_hi,
               dout, dq, dk, dv, gqk, gvp, sems):
        grad_middle = gm[...]
        branch = grad_middle.astype(BF16)
        for m in range(nmp):
            dout[:, m * lw : (m + 1) * lw] = nn(branch, wvp[m, :, lw : 2 * lw]).astype(BF16)
        mask = head_mask()
        ds_o[...] = jnp.zeros(ds_o.shape, F32)

        def one(w, carry):
            at = pl.ds(pl.multiple_of(w * PAD, PAD), PAD)
            for t in range(tiles):
                cols = slice(t * TILE, (t + 1) * TILE)
                p = probs[w * tiles + t]
                wide = spread(dout[at, cols], mask)
                dv[at, cols] = tn(p.astype(BF16), wide).astype(BF16)
                dp = nt(wide, v[at, cols])
                ds = p * (dp - jnp.sum(dp * p, axis=-1, keepdims=True))
                ds_o[t] = ds_o[t] + ds
                low = ds.astype(BF16)
                dq[at, cols] = (fold(nn(low, k[at, cols]), mask) * scale).astype(BF16)
                dk[at, cols] = (tn(low, spread(q[at, cols], mask)) * scale).astype(BF16)
            return carry

        lax.fori_loop(0, windows, one, 0)
        x = xw[...].astype(F32)
        unit, inverse = unit_of(x)
        xn = (unit * gs[0:1] + gs[2:3]).astype(BF16)
        back = jnp.zeros_like(x)
        for m in range(nmp):
            cols = slice(m * lw, (m + 1) * lw)
            gqk[m, :, 0:lw] = tn(xn, dq[:, cols]).astype(BF16)
            gqk[m, :, lw : 2 * lw] = tn(xn, dk[:, cols]).astype(BF16)
            gvp[m, :, 0:lw] = tn(xn, dv[:, cols]).astype(BF16)
            gvp[m, :, lw : 2 * lw] = tn(branch, mixed[:, cols]).astype(BF16)
            back = back + nt(dq[:, cols], wqk[m, :, 0:lw])
            back = back + nt(dk[:, cols], wqk[m, :, lw : 2 * lw])
            back = back + nt(dv[:, cols], wvp[m, :, 0:lw])
        a = store_slots(ids, deltas, gqk, (gqk_lo, gqk_hi), sems.at[0], rows)
        b = store_slots(ids, deltas, gvp, (gvp_lo, gvp_hi), sems.at[1], rows)
        d_img = grad_middle + norm_back(back, unit, inverse, gs[0:1])
        dimg_o[...] = tn(perm[...], d_img.astype(BF16)).astype(BF16)
        small_o[...] = jnp.zeros(small_o.shape, F32)
        small_o[0:1] = jnp.sum(back * unit, axis=0, keepdims=True)
        small_o[1:2] = jnp.sum(back, axis=0, keepdims=True)
        small_o[2:3] = jnp.sum(dq[...].astype(F32), axis=0, keepdims=True)
        small_o[3:4] = jnp.sum(dv[...].astype(F32), axis=0, keepdims=True)
        finish(a)
        finish(b)

    return kernel


VM = pl.BlockSpec(memory_space=pltpu.VMEM)
SM = pl.BlockSpec(memory_space=pltpu.SMEM)
HB = pl.BlockSpec(memory_space=pl.ANY)


def shape(dims, kind):
    return jax.ShapeDtypeStruct(dims, kind)


def solution(mesh):
    ndp, nmp = mesh.shape["dp"], mesh.shape["mp"]
    links = Links(ndp, nmp)
    deltas = links.deltas

    def body(images, cotangent, w_query, w_key, w_value, w_proj, w_up, w_down,
             gains, shifts, qv_bias, up_bias, table, regions, rel_index):
        held, tokens, width = images.shape
        rows = w_query.shape[0]
        lw = w_query.shape[1]
        fw = w_up.shape[1]
        heads = table.shape[0] * nmp
        codes = table.shape[1]
        windows = held * WINDOWS // nmp
        assert windows * nmp == held * WINDOWS
        taken = max(1, held // nmp)
        sharing = max(1, nmp // held)
        tiles = width // TILE
        r0 = windows * PAD
        raster = taken * tokens
        chunk = min(fw, 512)
        me_dp = lax.axis_index("dp")
        me_mp = lax.axis_index("mp")
        ids = jnp.stack([me_dp, me_mp]).astype(jnp.int32)

        extra = jnp.concatenate([gains, shifts], axis=0).T
        extra = jnp.pad(extra, ((0, 0), (0, 128 - extra.shape[1])))
        qk = links.gather(jnp.concatenate([w_query, w_key, extra], axis=1))
        vp = links.gather(jnp.concatenate([w_value, w_proj.T], axis=1))
        up = links.gather(w_up)
        dn = links.gather(w_down.T)
        flat = jnp.concatenate([qv_bias.reshape(-1), up_bias, table.reshape(-1)])
        flat = jnp.pad(flat, (0, -flat.shape[0] % 2048))
        both = links.over_mp(flat)
        both = jnp.concatenate(
            [lax.dynamic_slice_in_dim(both, me_mp ^ m, 1, 0) for m in range(nmp)], axis=0
        )
        qvb = both[:, : 2 * lw].reshape(nmp, 2, lw).transpose(1, 0, 2).reshape(2, nmp * lw)
        qvb = qvb.astype(F32)
        upb = both[:, 2 * lw : 2 * lw + fw].reshape(1, nmp * fw).astype(F32)
        full_table = both[:, 2 * lw + fw : 2 * lw + fw + table.size].reshape(heads, codes)

        gap = PAD - TOKENS
        codes_at = jnp.pad(rel_index, ((0, gap), (0, gap)), constant_values=-1)
        onehot = (codes_at.reshape(1, -1) == jnp.arange(codes, dtype=jnp.int32)[:, None]).astype(
            BF16
        )
        bias = jnp.dot(full_table, onehot, preferred_element_type=F32)
        bias = bias.reshape(heads * PAD, PAD)
        own = (me_mp * windows + jnp.arange(windows)) % WINDOWS
        area = jnp.pad(regions, ((0, 0), (0, gap)))[own]
        rmask = jnp.where(area[:, :, None] == area[:, None, :], 0.0, -100.0).astype(F32)
        rmask = jnp.where((jnp.arange(PAD) < TOKENS)[None, None, :], rmask, -1e30)

        r = jnp.arange(r0, dtype=jnp.int32)
        w = r // PAD
        at = r % PAD
        glob = me_mp * windows + w
        img = glob // WINDOWS - (me_mp // sharing) * taken
        wn = glob % WINDOWS
        gr = ((wn // 2) * WIN + at // WIN + SHIFT) % SIDE
        gc = ((wn % 2) * WIN + at % WIN + SHIFT) % SIDE
        token = jnp.where(at < TOKENS, img * tokens + gr * SIDE + gc, -1)
        perm = (token[:, None] == jnp.arange(raster, dtype=jnp.int32)[None, :]).astype(BF16)
        first = (me_mp // sharing) * taken
        mine = lax.dynamic_slice_in_dim(images, first, taken, 0).reshape(raster, width)
        cot = lax.dynamic_slice_in_dim(cotangent, first, taken, 0).reshape(raster, width)

        n = len(deltas)
        half = n // len(qk)
        params = pltpu.CompilerParams(vmem_limit_bytes=60 * 1024 * 1024)
        wide = 2 * lw + 128
        xw, q, k, v, probs, mixed, middle, gs, wqk, wvp = pl.pallas_call(
            attention_forward(deltas, nmp, lw, rows, windows, tiles),
            out_shape=(
                shape((r0, width), BF16), shape((r0, width), BF16), shape((r0, width), BF16),
                shape((r0, width), BF16), shape((windows * tiles, HPT * PAD, PAD), F32),
                shape((r0, width), BF16), shape((r0, width), F32), shape((8, width), F32),
                shape((nmp, width, wide), BF16), shape((nmp, width, 2 * lw), BF16),
            ),
            in_specs=[SM, VM, VM, HB, HB, HB, HB, VM, VM, VM],
            out_specs=(VM,) * 10,
            scratch_shapes=[pltpu.SemaphoreType.DMA((2, n))],
            compiler_params=params,
            name="attention_forward",
        )(ids, mine, perm, *qk, *vp, qvb, bias, rmask)

        grads = (half, rows, fw)
        out_img, gm, small_two, gup_lo, gup_hi, gdn_lo, gdn_hi = pl.pallas_call(
            feed_forward(deltas, nmp, fw, rows, chunk),
            out_shape=(
                shape((raster, width), BF16), shape((r0, width), F32), shape((8, width), F32),
            ) + (shape(grads, BF16),) * 4,
            in_specs=[SM, VM, VM, VM, VM, HB, HB, HB, HB, VM],
            out_specs=(VM, VM, VM, HB, HB, HB, HB),
            scratch_shapes=[pltpu.VMEM((nmp, width, fw), BF16)] * 4
            + [pltpu.SemaphoreType.DMA((2, n))],
            compiler_params=params,
            name="feed_forward",
        )(ids, cot, perm, middle, gs, *up, *dn, upb)

        grads = (half, rows, 2 * lw)
        d_img, small_one, ds, gqk_lo, gqk_hi, gvp_lo, gvp_hi = pl.pallas_call(
            attention_backward(deltas, nmp, lw, rows, windows, tiles),
            out_shape=(
                shape((raster, width), BF16), shape((8, width), F32),
                shape((tiles, HPT * PAD, PAD), F32),
            ) + (shape(grads, BF16),) * 4,
            in_specs=[SM] + [VM] * 11,
            out_specs=(VM, VM, VM, HB, HB, HB, HB),
            scratch_shapes=[pltpu.VMEM((r0, width), BF16)] * 4
            + [pltpu.VMEM((nmp, width, 2 * lw), BF16)] * 2
            + [pltpu.SemaphoreType.DMA((2, n))],
            compiler_params=params,
            name="attention_backward",
        )(ids, xw, perm, wqk, wvp, q, k, v, probs, mixed, gm, gs)

        def whole(x):
            bit = 1
            while bit < sharing:
                x = x + links.swap(x, (0, bit))
                bit *= 2
            x = x.reshape(taken, tokens, width)
            while bit < nmp:
                other = links.swap(x, (0, bit))
                upper = (me_mp & bit) != 0
                x = jnp.concatenate(
                    [jnp.where(upper, other, x), jnp.where(upper, x, other)], axis=0
                )
                bit *= 2
            return x

        output = whole(out_img)
        d_images = whole(d_img)
        g_up = links.scatter([gup_lo, gup_hi])
        g_down = links.scatter([gdn_lo, gdn_hi]).T
        g_vp = links.scatter([gvp_lo, gvp_hi])
        g_qk = links.scatter([gqk_lo, gqk_hi])
        g_table = lax.dot_general(
            ds.reshape(heads, PAD * PAD), onehot.astype(F32), (((1,), (1,)), ((), ())),
            precision=lax.Precision.HIGHEST,
        )
        packed = jnp.concatenate(
            [small_one, small_two, jnp.pad(g_table, ((0, 0), (0, width - codes)))], axis=0
        )
        packed = links.total(packed)
        cut = lax.dynamic_slice_in_dim(packed[:16], me_dp * rows, rows, 1)
        g_gains = jnp.stack([cut[0], cut[8]])
        g_shifts = jnp.stack([cut[1], cut[9], cut[10], cut[11]])
        g_qv = lax.dynamic_slice_in_dim(packed[2:4], me_mp * lw, lw, 1)
        g_upb = lax.dynamic_slice_in_dim(packed[12:16].reshape(-1), me_mp * fw, fw, 0)
        g_tab = lax.dynamic_slice_in_dim(packed[16:], me_mp * table.shape[0], table.shape[0], 0)
        return (
            output, d_images, g_qk[:, :lw], g_qk[:, lw:], g_vp[:, :lw], g_vp[:, lw:].T,
            g_up, g_down, g_gains, g_shifts, g_qv, g_upb, g_tab[:, :codes],
        )

    return jax.shard_map(
        body,
        mesh=mesh,
        in_specs=(
            P("dp", None, None),
            P("dp", None, None),
            P("dp", "mp"),
            P("dp", "mp"),
            P("dp", "mp"),
            P("mp", "dp"),
            P("dp", "mp"),
            P("mp", "dp"),
            P(None, "dp"),
            P(None, "dp"),
            P(None, "mp"),
            P("mp"),
            P("mp", None),
            P(),
            P(),
        ),
        out_specs=(
            P("dp", None, None),
            P("dp", None, None),
            P("dp", "mp"),
            P("dp", "mp"),
            P("dp", "mp"),
            P("mp", "dp"),
            P("dp", "mp"),
            P("mp", "dp"),
            P(None, "dp"),
            P(None, "dp"),
            P(None, "mp"),
            P("mp"),
            P("mp", None),
        ),
        check_vma=False,
    )
```

```python
import math

import jax
import jax.numpy as jnp
from jax import lax
from jax.experimental import pallas as pl
from jax.experimental.pallas import tpu as pltpu
from jax.sharding import PartitionSpec as P


HEAD_DIM = 32
SIDE = 14
WIN = 7
SHIFT = 3
WINDOWS = 4
TOKENS = WIN * WIN
PAD = 64
TILE = 128
HPT = TILE // HEAD_DIM
F32 = jnp.float32
BF16 = jnp.bfloat16
AXES = ("dp", "mp")


def nn(a, b):
    return lax.dot_general(a, b, (((1,), (0,)), ((), ())), preferred_element_type=F32)


def nt(a, b):
    return lax.dot_general(a, b, (((1,), (1,)), ((), ())), preferred_element_type=F32)


def tn(a, b):
    return lax.dot_general(a, b, (((0,), (0,)), ((), ())), preferred_element_type=F32)


def unit_of(v):
    centred = v - jnp.mean(v, axis=-1, keepdims=True)
    inverse = lax.rsqrt(jnp.mean(centred * centred, axis=-1, keepdims=True) + 1e-05)
    return centred * inverse, inverse


def norm_back(grad_in, unit_rows, inverse, gain_row):
    scaled = grad_in * gain_row
    return inverse * (
        scaled
        - jnp.mean(scaled, axis=-1, keepdims=True)
        - unit_rows * jnp.mean(scaled * unit_rows, axis=-1, keepdims=True)
    )


class Links:
    def __init__(self, ndp, nmp, mp_first):
        self.ndp, self.nmp = ndp, nmp
        dp_bits = [1 << b for b in range(ndp.bit_length() - 1)]
        mp_bits = [1 << b for b in range(nmp.bit_length() - 1)]
        stages = []
        high = dp_bits[2:]
        while high:
            stages.append(self.combos([(b, 0) for b in high[-2:]]))
            high = high[:-2]
        near = [[(dp_bits[1], 0)]] if len(dp_bits) > 1 else []
        across = []
        left = list(mp_bits)
        while left:
            across.append(self.combos([(0, b) for b in left[:2]]))
            left = left[2:]
        stages += across + near if mp_first else near + across
        if dp_bits:
            stages.append([(dp_bits[0], 0)])
        self.stages = stages
        deltas = [(0, 0)]
        for group in stages:
            deltas = deltas + [(a ^ o[0], b ^ o[1]) for o in group for a, b in deltas]
        self.deltas = deltas

    @staticmethod
    def combos(gens):
        out = [(0, 0)]
        for g in gens:
            out = out + [(a ^ g[0], b ^ g[1]) for a, b in out]
        return out[1:]

    def swap(self, x, offset):
        pairs = []
        for d in range(self.ndp):
            for m in range(self.nmp):
                pairs.append(
                    (d * self.nmp + m, (d ^ offset[0]) * self.nmp + (m ^ offset[1]))
                )
        return lax.ppermute(x, AXES, pairs)

    def gather(self, block):
        buf = block[None]
        for group in self.stages[:-2]:
            buf = jnp.concatenate([buf] + [self.swap(buf, o) for o in group], axis=0)
        parts = [buf] + [self.swap(buf, o) for o in self.stages[-2]]
        return parts + [self.swap(p, o) for o in self.stages[-1] for p in parts]

    def scatter_step(self, parts, at):
        got = [self.swap(p, o) for p, o in zip(parts[1:], self.stages[at])]
        if at == 0:
            total = parts[0].astype(F32)
            for g in got:
                total = total + g.astype(F32)
            return total[0]
        blocks = len(self.stages[at - 1]) + 1
        n = parts[0].shape[0] // blocks
        fresh = []
        for b in range(blocks):
            piece = parts[0][b * n : (b + 1) * n].astype(F32)
            for g in got:
                piece = piece + g[b * n : (b + 1) * n].astype(F32)
            fresh.append(piece.astype(BF16))
        return fresh

    def scatter_rest(self, parts):
        for at in range(len(self.stages) - 2, -1, -1):
            parts = self.scatter_step(parts, at)
        return parts

    def total(self, x):
        for group in reversed(self.stages):
            got = [self.swap(x, o) for o in group]
            for g in got:
                x = x + g
        return x

    def over_mp(self, x):
        buf = x[None]
        bit = 1
        while bit < self.nmp:
            buf = jnp.concatenate([buf, self.swap(buf, (0, bit))], axis=0)
            bit *= 2
        return buf


def load_slots(ids, deltas, pieces, dst, sems, rows):
    per = len(deltas) // len(pieces)
    copies = []
    for j, (dd, dm) in enumerate(deltas):
        d = lax.bitwise_xor(ids[0], dd)
        m = lax.bitwise_xor(ids[1], dm)
        copies.append(
            pltpu.make_async_copy(
                pieces[j // per].at[j % per],
                dst.at[m, pl.ds(pl.multiple_of(d * rows, rows), rows), :],
                sems.at[j],
            )
        )
    for c in copies:
        c.start()
    return copies


def store_slots(ids, deltas, src, pieces, sems, rows):
    per = len(deltas) // len(pieces)
    copies = []
    for j, (dd, dm) in enumerate(deltas):
        d = lax.bitwise_xor(ids[0], dd)
        m = lax.bitwise_xor(ids[1], dm)
        copies.append(
            pltpu.make_async_copy(
                src.at[m, pl.ds(pl.multiple_of(d * rows, rows), rows), :],
                pieces[j // per].at[j % per],
                sems.at[j],
            )
        )
    for c in copies:
        c.start()
    return copies


def finish(copies):
    for c in copies:
        c.wait()


def head_mask():
    row = lax.broadcasted_iota(jnp.int32, (HPT * PAD, TILE), 0) // PAD
    lane = lax.broadcasted_iota(jnp.int32, (HPT * PAD, TILE), 1) // HEAD_DIM
    return row == lane


def spread(x, mask):
    stacked = jnp.concatenate([x] * HPT, axis=0)
    return jnp.where(mask, stacked, jnp.zeros_like(stacked))


def fold(x, mask):
    x = jnp.where(mask, x, 0.0)
    out = x[:PAD]
    for h in range(1, HPT):
        out = out + x[h * PAD : (h + 1) * PAD]
    return out


def attention_forward(deltas, count, nmp, lw, rows, windows, tiles):
    scale = HEAD_DIM**-0.5

    def kernel(ids, x_img, perm, qvb, bias, rmask, *rest):
        pieces, rest = rest[:count], rest[count:]
        xw_o, q_o, k_o, v_o, p_o, mixed_o, middle_o, gs_o, wat, sems = rest
        a = load_slots(ids, deltas, pieces, wat, sems, rows)
        xw = nn(perm[...], x_img[...])
        xw_o[...] = xw.astype(BF16)
        unit, _ = unit_of(xw)
        finish(a)
        gs = wat[0, :, 4 * lw : 4 * lw + 128].astype(F32).T
        gs_o[...] = gs[:8]
        xn = (unit * gs[0:1] + gs[2:3]).astype(BF16)
        for m in range(nmp):
            cols = slice(m * lw, (m + 1) * lw)
            q_o[:, cols] = (nn(xn, wat[m, :, 0:lw]) + qvb[0:1, cols]).astype(BF16)
            k_o[:, cols] = nn(xn, wat[m, :, lw : 2 * lw]).astype(BF16)
            v_o[:, cols] = (nn(xn, wat[m, :, 2 * lw : 3 * lw]) + qvb[1:2, cols]).astype(BF16)
        mask = head_mask()

        def one(w, carry):
            at = pl.ds(pl.multiple_of(w * PAD, PAD), PAD)
            area = jnp.concatenate([rmask[w]] * HPT, axis=0)
            for t in range(tiles):
                cols = slice(t * TILE, (t + 1) * TILE)
                raw = nt(spread(q_o[at, cols], mask), k_o[at, cols])
                logits = raw * scale + bias[t * HPT * PAD : (t + 1) * HPT * PAD, :] + area
                top = jnp.max(logits, axis=-1, keepdims=True)
                e = jnp.exp(logits - top)
                probs = e / jnp.sum(e, axis=-1, keepdims=True)
                p_o[w * tiles + t] = probs
                got = nn(probs.astype(BF16), v_o[at, cols])
                mixed_o[at, cols] = fold(got, mask).astype(BF16)
            return carry

        lax.fori_loop(0, windows, one, 0)
        total = xw + gs[4:5]
        for m in range(nmp):
            total = total + nt(mixed_o[:, m * lw : (m + 1) * lw], wat[m, :, 3 * lw : 4 * lw])
        middle_o[...] = total

    return kernel


def feed_forward(deltas, count, nmp, fw, rows, chunk):
    root = 1.0 / math.sqrt(2.0)
    root_pi = 1.0 / math.sqrt(2.0 * math.pi)

    def kernel(ids, cot_img, perm, middle, gs, upb, *rest):
        pieces, rest = rest[:count], rest[count:]
        out_o, gm_o, small_o, g_lo, g_hi, wff, gff, sems = rest
        a = load_slots(ids, deltas, pieces, wff, sems, rows)
        cot = nn(perm[...], cot_img[...])
        cot_low = cot.astype(BF16)
        mid = middle[...]
        unit, inverse = unit_of(mid)
        normed = (unit * gs[1:2] + gs[3:4]).astype(BF16)
        finish(a)
        out = mid + gs[5:6]
        lifted = jnp.zeros_like(mid)
        small_o[...] = jnp.zeros(small_o.shape, F32)
        for m in range(nmp):
            for c in range(0, fw, chunk):
                cols = slice(c, c + chunk)
                down = slice(fw + c, fw + c + chunk)
                first = m * fw + c
                hidden = nn(normed, wff[m, :, cols]) + upb[0:1, first : first + chunk]
                cdf = 0.5 * (1.0 + lax.erf(hidden * root))
                active = (hidden * cdf).astype(BF16)
                slope = cdf + hidden * (jnp.exp(-0.5 * hidden * hidden) * root_pi)
                out = out + nt(active, wff[m, :, down])
                gh32 = nn(cot_low, wff[m, :, down]) * slope
                gh = gh32.astype(BF16)
                lifted = lifted + nt(gh, wff[m, :, cols])
                gff[m, :, cols] = tn(normed, gh).astype(BF16)
                gff[m, :, down] = tn(cot_low, active).astype(BF16)
                small_o[4 + first // 512 : 5 + first // 512, first % 512 : first % 512 + chunk] = (
                    jnp.sum(gh.astype(F32), axis=0, keepdims=True)
                )
        a = store_slots(ids, deltas, gff, (g_lo, g_hi), sems, rows)
        out_o[...] = tn(perm[...], out.astype(BF16)).astype(BF16)
        gm = cot + norm_back(lifted, unit, inverse, gs[1:2])
        gm_o[...] = gm
        small_o[0:1] = jnp.sum(lifted * unit, axis=0, keepdims=True)
        small_o[1:2] = jnp.sum(lifted, axis=0, keepdims=True)
        small_o[2:3] = jnp.sum(gm, axis=0, keepdims=True)
        small_o[3:4] = jnp.sum(cot, axis=0, keepdims=True)
        finish(a)

    return kernel


def attention_backward(nmp, lw, windows, tiles):
    scale = HEAD_DIM**-0.5

    def kernel(wat, q, k, v, probs, gm, dq, dk, dv, ds_o, dout):
        branch = gm[...].astype(BF16)
        for m in range(nmp):
            proj = wat[m, :, 3 * lw : 4 * lw]
            dout[:, m * lw : (m + 1) * lw] = nn(branch, proj).astype(BF16)
        mask = head_mask()
        ds_o[...] = jnp.zeros(ds_o.shape, F32)

        def one(w, carry):
            at = pl.ds(pl.multiple_of(w * PAD, PAD), PAD)
            for t in range(tiles):
                cols = slice(t * TILE, (t + 1) * TILE)
                p = probs[w * tiles + t]
                wide = spread(dout[at, cols], mask)
                dv[at, cols] = tn(p.astype(BF16), wide).astype(BF16)
                dp = nt(wide, v[at, cols])
                ds = p * (dp - jnp.sum(dp * p, axis=-1, keepdims=True))
                ds_o[t] = ds_o[t] + ds
                low = ds.astype(BF16)
                dq[at, cols] = (fold(nn(low, k[at, cols]), mask) * scale).astype(BF16)
                dk[at, cols] = (tn(low, spread(q[at, cols], mask)) * scale).astype(BF16)
            return carry

        lax.fori_loop(0, windows, one, 0)

    return kernel


def attention_weights(deltas, nmp, lw, rows):
    def kernel(ids, xw, perm, wat, mixed, gm, gs, dq, dk, dv,
               dimg_o, small_o, g_lo, g_hi, gat, sems):
        grad_middle = gm[...]
        branch = grad_middle.astype(BF16)
        x = xw[...].astype(F32)
        unit, inverse = unit_of(x)
        xn = (unit * gs[0:1] + gs[2:3]).astype(BF16)
        for m in range(nmp):
            cols = slice(m * lw, (m + 1) * lw)
            gat[m, :, 0:lw] = tn(xn, dq[:, cols]).astype(BF16)
            gat[m, :, lw : 2 * lw] = tn(xn, dk[:, cols]).astype(BF16)
            gat[m, :, 2 * lw : 3 * lw] = tn(xn, dv[:, cols]).astype(BF16)
            gat[m, :, 3 * lw : 4 * lw] = tn(branch, mixed[:, cols]).astype(BF16)
        a = store_slots(ids, deltas, gat, (g_lo, g_hi), sems, rows)
        back = jnp.zeros_like(x)
        for m in range(nmp):
            cols = slice(m * lw, (m + 1) * lw)
            back = back + nt(dq[:, cols], wat[m, :, 0:lw])
            back = back + nt(dk[:, cols], wat[m, :, lw : 2 * lw])
            back = back + nt(dv[:, cols], wat[m, :, 2 * lw : 3 * lw])
        d_img = grad_middle + norm_back(back, unit, inverse, gs[0:1])
        dimg_o[...] = tn(perm[...], d_img.astype(BF16)).astype(BF16)
        small_o[...] = jnp.zeros(small_o.shape, F32)
        small_o[0:1] = jnp.sum(back * unit, axis=0, keepdims=True)
        small_o[1:2] = jnp.sum(back, axis=0, keepdims=True)
        small_o[2:3] = jnp.sum(dq[...].astype(F32), axis=0, keepdims=True)
        small_o[3:4] = jnp.sum(dv[...].astype(F32), axis=0, keepdims=True)
        finish(a)

    return kernel


VM = pl.BlockSpec(memory_space=pltpu.VMEM)
SM = pl.BlockSpec(memory_space=pltpu.SMEM)
HB = pl.BlockSpec(memory_space=pl.ANY)


def shape(dims, kind):
    return jax.ShapeDtypeStruct(dims, kind)


def solution(mesh):
    ndp, nmp = mesh.shape["dp"], mesh.shape["mp"]
    links = Links(ndp, nmp, False)
    links_ff = Links(ndp, nmp, True)
    deltas = links.deltas

    def body(images, cotangent, w_query, w_key, w_value, w_proj, w_up, w_down,
             gains, shifts, qv_bias, up_bias, table, regions, rel_index):
        held, tokens, width = images.shape
        rows = w_query.shape[0]
        lw = w_query.shape[1]
        fw = w_up.shape[1]
        heads = table.shape[0] * nmp
        codes = table.shape[1]
        windows = held * WINDOWS // nmp
        assert windows * nmp == held * WINDOWS
        taken = max(1, held // nmp)
        sharing = max(1, nmp // held)
        tiles = width // TILE
        r0 = windows * PAD
        raster = taken * tokens
        chunk = min(fw, 512)
        me_dp = lax.axis_index("dp")
        me_mp = lax.axis_index("mp")
        ids = jnp.stack([me_dp, me_mp]).astype(jnp.int32)

        extra = jnp.concatenate([gains, shifts], axis=0).T
        extra = jnp.pad(extra, ((0, 0), (0, 128 - extra.shape[1])))
        at_w = links.gather(
            jnp.concatenate([w_query, w_key, w_value, w_proj.T, extra], axis=1)
        )
        ff_w = links_ff.gather(jnp.concatenate([w_up, w_down.T], axis=1))
        flat = jnp.concatenate([qv_bias.reshape(-1), up_bias, table.reshape(-1)])
        flat = jnp.pad(flat, (0, -flat.shape[0] % 2048))
        both = links.over_mp(flat)
        both = jnp.concatenate(
            [lax.dynamic_slice_in_dim(both, me_mp ^ m, 1, 0) for m in range(nmp)], axis=0
        )
        qvb = both[:, : 2 * lw].reshape(nmp, 2, lw).transpose(1, 0, 2).reshape(2, nmp * lw)
        qvb = qvb.astype(F32)
        upb = both[:, 2 * lw : 2 * lw + fw].reshape(1, nmp * fw).astype(F32)
        full_table = both[:, 2 * lw + fw : 2 * lw + fw + table.size].reshape(heads, codes)

        gap = PAD - TOKENS
        codes_at = jnp.pad(rel_index, ((0, gap), (0, gap)), constant_values=-1)
        onehot = (codes_at.reshape(1, -1) == jnp.arange(codes, dtype=jnp.int32)[:, None]).astype(
            BF16
        )
        bias = jnp.dot(full_table, onehot, preferred_element_type=F32)
        bias = bias.reshape(heads * PAD, PAD)
        own = (me_mp * windows + jnp.arange(windows)) % WINDOWS
        area = jnp.pad(regions, ((0, 0), (0, gap)))[own]
        rmask = jnp.where(area[:, :, None] == area[:, None, :], 0.0, -100.0).astype(F32)
        rmask = jnp.where((jnp.arange(PAD) < TOKENS)[None, None, :], rmask, -1e30)

        r = jnp.arange(r0, dtype=jnp.int32)
        w = r // PAD
        at = r % PAD
        glob = me_mp * windows + w
        img = glob // WINDOWS - (me_mp // sharing) * taken
        wn = glob % WINDOWS
        gr = ((wn // 2) * WIN + at // WIN + SHIFT) % SIDE
        gc = ((wn % 2) * WIN + at % WIN + SHIFT) % SIDE
        token = jnp.where(at < TOKENS, img * tokens + gr * SIDE + gc, -1)
        perm = (token[:, None] == jnp.arange(raster, dtype=jnp.int32)[None, :]).astype(BF16)
        first = (me_mp // sharing) * taken
        mine = lax.dynamic_slice_in_dim(images, first, taken, 0).reshape(raster, width)
        cot = lax.dynamic_slice_in_dim(cotangent, first, taken, 0).reshape(raster, width)

        n = len(deltas)

        def call(fn, micros, out, in_specs, out_specs, scratch):
            return pl.pallas_call(
                fn, out_shape=out, in_specs=in_specs, out_specs=out_specs,
                scratch_shapes=scratch,
                compiler_params=pltpu.CompilerParams(vmem_limit_bytes=60 * 1024 * 1024),
                cost_estimate=pl.CostEstimate(
                    flops=int(micros * 1e9), bytes_accessed=int(micros * 3.5e6),
                    transcendentals=0,
                ),
            )

        full = shape((r0, width), BF16)
        wide = 4 * lw + 128
        xw, q, k, v, probs, mixed, middle, gs, wat = call(
            attention_forward(deltas, len(at_w), nmp, lw, rows, windows, tiles),
            15,
            (
                full, full, full, full, shape((windows * tiles, HPT * PAD, PAD), F32),
                full, shape((r0, width), F32), shape((8, width), F32),
                shape((nmp, width, wide), BF16),
            ),
            [SM] + [VM] * 5 + [HB] * len(at_w),
            (VM,) * 9,
            [pltpu.SemaphoreType.DMA((n,))],
        )(ids, mine, perm, qvb, bias, rmask, *at_w)

        grads = shape((n // 2, rows, 2 * fw), BF16)
        out_img, gm, small_two, gff_lo, gff_hi = call(
            feed_forward(links_ff.deltas, len(ff_w), nmp, fw, rows, chunk),
            15,
            (shape((raster, width), BF16), shape((r0, width), F32), shape((8, width), F32),
             grads, grads),
            [SM] + [VM] * 5 + [HB] * len(ff_w),
            (VM, VM, VM, HB, HB),
            [pltpu.VMEM((nmp, width, 2 * fw), BF16)] * 2 + [pltpu.SemaphoreType.DMA((n,))],
        )(ids, cot, perm, middle, gs, upb, *ff_w)

        def whole(x):
            bit = 1
            while bit < sharing:
                x = x + links.swap(x, (0, bit))
                bit *= 2
            x = x.reshape(taken, tokens, width)
            while bit < nmp:
                other = links.swap(x, (0, bit))
                upper = (me_mp & bit) != 0
                x = jnp.concatenate(
                    [jnp.where(upper, other, x), jnp.where(upper, x, other)], axis=0
                )
                bit *= 2
            return x

        output = whole(out_img)
        last = len(links.stages) - 1
        ff_parts = links_ff.scatter_step([gff_lo, gff_hi], last)

        dq, dk, dv, ds = call(
            attention_backward(nmp, lw, windows, tiles),
            12,
            (full, full, full, shape((tiles, HPT * PAD, PAD), F32)),
            [VM] * 6,
            (VM,) * 4,
            [pltpu.VMEM((r0, width), BF16)],
        )(wat, q, k, v, probs, gm)

        dq, dk, dv, output, *ff_parts = lax.optimization_barrier(
            (dq, dk, dv, output, *ff_parts)
        )
        grads = shape((n // 2, rows, 4 * lw), BF16)
        g_ff = links_ff.scatter_rest(ff_parts)
        weights_call = call(
            attention_weights(deltas, nmp, lw, rows),
            8,
            (shape((raster, width), BF16), shape((8, width), F32), grads, grads),
            [SM] + [VM] * 9,
            (VM, VM, HB, HB),
            [pltpu.VMEM((nmp, width, 4 * lw), BF16), pltpu.SemaphoreType.DMA((n,))],
        )
        d_img, small_one, gat_lo, gat_hi = weights_call(
            ids, xw, perm, wat, mixed, gm, gs, dq, dk, dv
        )

        at_parts = links.scatter_step([gat_lo, gat_hi], last)
        d_images = whole(d_img)
        g_at = links.scatter_rest(at_parts)
        g_table = lax.dot_general(
            ds.reshape(heads, PAD * PAD), onehot.astype(F32), (((1,), (1,)), ((), ())),
            precision=lax.Precision.HIGHEST,
        )
        packed = jnp.concatenate(
            [small_one, small_two, jnp.pad(g_table, ((0, 0), (0, width - codes)))], axis=0
        )
        packed, *_ = lax.optimization_barrier((packed, *at_parts))
        packed = links.total(packed)
        cut = lax.dynamic_slice_in_dim(packed[:16], me_dp * rows, rows, 1)
        g_gains = jnp.stack([cut[0], cut[8]])
        g_shifts = jnp.stack([cut[1], cut[9], cut[10], cut[11]])
        g_qv = lax.dynamic_slice_in_dim(packed[2:4], me_mp * lw, lw, 1)
        g_upb = lax.dynamic_slice_in_dim(packed[12:16].reshape(-1), me_mp * fw, fw, 0)
        g_tab = lax.dynamic_slice_in_dim(packed[16:], me_mp * table.shape[0], table.shape[0], 0)
        return (
            output, d_images, g_at[:, :lw], g_at[:, lw : 2 * lw], g_at[:, 2 * lw : 3 * lw],
            g_at[:, 3 * lw :].T, g_ff[:, :fw], g_ff[:, fw:].T, g_gains, g_shifts, g_qv, g_upb, g_tab[:, :codes],
        )

    return jax.shard_map(
        body,
        mesh=mesh,
        in_specs=(
            P("dp", None, None),
            P("dp", None, None),
            P("dp", "mp"),
            P("dp", "mp"),
            P("dp", "mp"),
            P("mp", "dp"),
            P("dp", "mp"),
            P("mp", "dp"),
            P(None, "dp"),
            P(None, "dp"),
            P(None, "mp"),
            P("mp"),
            P("mp", None),
            P(),
            P(),
        ),
        out_specs=(
            P("dp", None, None),
            P("dp", None, None),
            P("dp", "mp"),
            P("dp", "mp"),
            P("dp", "mp"),
            P("mp", "dp"),
            P("dp", "mp"),
            P("mp", "dp"),
            P(None, "dp"),
            P(None, "dp"),
            P(None, "mp"),
            P("mp"),
            P("mp", None),
        ),
        check_vma=False,
    )
```
